32 devices in a mesh: grp: 2 (over y), ia: 4 (over x, core), ja: 4 (over z).
Axes of the slice: x: 2, y: 2, z: 4, core: 2. Of those that a mesh axis runs over, the one named last changes fastest.
Arguments:
- amplitudes: float32 [16, 8, 160, 160], P(('grp', 'ia'), 'ja'), parts along dimension 0, may hold values from -3 to 3
- integrals: float32 [16, 8, 160, 160], P(('grp', 'ia'), 'ja'), parts along dimension 0, may hold values from -6 to 6
- row_intersection: float32 [16, 8, 8, 160, 160], P(('grp', 'ia'), 'ja'), parts along dimension 0, as said below
- column_intersection: float32 [16, 8, 8, 160, 160], P(('grp', 'ia'), 'ja'), parts along dimension 0, as said below
- row_tiles: int32 [16, 8], P(('grp', 'ia')), parts along dimension 0, may hold values from 0 to 7, as said below
- row_coupling: float32 [16, 8], P(('grp', 'ia')), parts along dimension 0, may hold values from 0.02 to 0.12
- row_counts: int32 [16], P(('grp', 'ia')), parts along dimension 0, may hold values from 1 to 8, as said below
- column_tiles: int32 [16, 8], P(('grp', 'ja')), parts along dimension 0, may hold values from 0 to 7, as said below
- column_coupling: float32 [16, 8], P(('grp', 'ja')), parts along dimension 0, may hold values from 0.02 to 0.12
- column_counts: int32 [16], P(('grp', 'ja')), parts along dimension 0, may hold values from 1 to 8, as said below
- virtual_energy: float32 [16, 8, 160], P(('grp', 'ia'), 'ja'), parts along dimension 0, may hold values from 0.5 to 3
- first_energy: float32 [16], P(('grp', 'ia')), parts along dimension 0, may hold values from -1.5 to -0.3
- second_energy: float32 [16], P(('grp', 'ja')), parts along dimension 0, may hold values from -1.5 to -0.3
Outputs:
- new_amplitudes: float32 [16, 8, 160, 160], P(('grp', 'ia'), 'ja'), parts along dimension 0
- last_residual: float32 [16, 8, 160, 160], P(('grp', 'ia'), 'ja'), parts along dimension 0
The draws below stay inside these ranges and needn't reach their ends.
There are 2 independent parts, one for each index of `grp`. The reference program is written for one: setup_inputs(seed, part) draws one part's arguments, and reference() takes and returns one part's arrays. A program takes and returns all parts, laid end to end along the dimension named above; each array names one. Nothing has to cross between parts.
Inputs may be any that keep to these rules, and one draw needn't show every extreme that they name: `row_tiles`: each row holds 8 different first-fragment orbitals. `column_tiles`: each row holds 8 different second-fragment orbitals. `row_counts`: some orbital has all 8 slots live. `column_counts`: some orbital has all 8 slots live. `row_intersection`: identity plus an independent perturbation of full rank. `column_intersection`: identity plus an independent perturbation of full rank.
All inputs are finite; a program needn't handle non-finite values.
Results may differ from the reference program's by a relative error of at most 0.00017.
Values sent between devices are 32-bit elements; how exact they have to be, the bound alone decides.
No kernel may reach another device: no remote copies, remote signals or barrier semaphores. Data moves between devices by JAX's collectives and lax.ppermute only.
A program may use at most 128 MiB of HBM per device.

```python
import math
import jax
import jax.numpy as jnp
from jax import lax

P_SIZE = 160
ITERS = 2
NI = 8
NJ = 8
KL = 8


def intersection_draw(key):
    shape = (NI, NJ, KL, P_SIZE, P_SIZE)
    spread = 0.4 / P_SIZE ** 0.5
    noise = jax.random.normal(key, shape, jnp.float32) * spread
    return noise + jnp.eye(P_SIZE, dtype=jnp.float32)


def draw_row_intersection(key, part):
    return intersection_draw(jax.random.fold_in(key, 11))


def draw_column_intersection(key, part):
    return intersection_draw(jax.random.fold_in(key, 13))


def tile_lists(key, total):
    keys = jax.random.split(key, total)
    return jax.vmap(lambda single: jax.random.permutation(single, total)[:KL])(keys).astype(jnp.int32)


def draw_row_tiles(key, part):
    return tile_lists(jax.random.fold_in(key, 21), NI)


def draw_column_tiles(key, part):
    return tile_lists(jax.random.fold_in(key, 23), NJ)


def live_counts(key, total):
    first, second = jax.random.split(key)
    counts = jax.random.randint(first, (total,), 1, KL + 1, dtype=jnp.int32)
    where = jax.random.randint(second, (), 0, total, dtype=jnp.int32)
    return counts.at[where].set(KL)


def draw_row_counts(key, part):
    return live_counts(jax.random.fold_in(key, 31), NI)


def draw_column_counts(key, part):
    return live_counts(jax.random.fold_in(key, 33), NJ)


def shard_levels(stream_key, extent, cuts, least, top_value):
    def one(dim, shards_of):
        draws = jax.random.uniform(jax.random.fold_in(jax.random.fold_in(stream_key, 6), dim), (shards_of,), jnp.float32, least / len(cuts), top_value / len(cuts))
        return jnp.repeat(jnp.exp(draws), extent[dim] // shards_of).reshape((-1,) + (1,) * (len(extent) - dim - 1))

    factor_of = one(*cuts[0])
    for cut in cuts[1:]:
        factor_of = factor_of * one(*cut)
    return factor_of


def scatter_about(stream_key, extent, scale, bound, pieces=(), kind=jnp.bfloat16):
    entries = jax.random.normal(stream_key, extent, jnp.float32) * scale
    if len(pieces) > 0:
        entries = shard_levels(stream_key, extent, pieces, -0.22, 0.18) * entries
    return jnp.clip(entries, min=-bound, max=bound).astype(kind)


def setup_inputs(seed: int = 0, part: int = 0) -> dict:
    arg_keys = jax.random.split(jax.random.key(seed), 14)
    own_keys = jax.random.split(jax.random.fold_in(arg_keys[13], part), 14)
    amplitudes = scatter_about(own_keys[0], (NI, NJ, P_SIZE, P_SIZE), 0.5, 3.0, ((0, 4), (1, 4)), jnp.float32)
    integrals = scatter_about(own_keys[1], (NI, NJ, P_SIZE, P_SIZE), 1.0, 6.0, ((0, 4), (1, 4)), jnp.float32)
    row_intersection = draw_row_intersection(jax.random.fold_in(jax.random.fold_in(arg_keys[13], part), 71), part)
    column_intersection = draw_column_intersection(jax.random.fold_in(jax.random.fold_in(arg_keys[13], part), 71), part)
    row_tiles = draw_row_tiles(jax.random.fold_in(jax.random.fold_in(arg_keys[13], part), 71), part)
    row_coupling = jnp.clip(jnp.exp(math.log(0.12) - 1.7917595 * jax.random.uniform(own_keys[5], (NI, KL), jnp.float32) ** shard_levels(own_keys[5], (NI, KL), ((0, 4),), -0.2, 0.2)), 0.02, 0.12)
    row_counts = draw_row_counts(jax.random.fold_in(jax.random.fold_in(arg_keys[13], part), 71), part)
    column_tiles = draw_column_tiles(jax.random.fold_in(jax.random.fold_in(arg_keys[13], part), 71), part)
    column_coupling = jnp.clip(jnp.exp(math.log(0.12) - 1.7917595 * jax.random.uniform(own_keys[8], (NJ, KL), jnp.float32) ** shard_levels(own_keys[8], (NJ, KL), ((0, 4),), -0.2, 0.2)), 0.02, 0.12)
    column_counts = draw_column_counts(jax.random.fold_in(jax.random.fold_in(arg_keys[13], part), 71), part)
    virtual_energy = jnp.clip(0.5 + 2.5 * jax.random.uniform(own_keys[10], (NI, NJ, P_SIZE), jnp.float32) ** shard_levels(own_keys[10], (NI, NJ, P_SIZE), ((0, 4), (1, 4)), -0.2, 0.2), 0.5, 3.0)
    first_energy = jnp.clip(-1.5 + 1.2 * jax.random.uniform(own_keys[11], (NI,), jnp.float32) ** shard_levels(own_keys[11], (NI,), ((0, 4),), -0.2, 0.2), -1.5, -0.3)
    second_energy = jnp.clip(-1.5 + 1.2 * jax.random.uniform(own_keys[12], (NJ,), jnp.float32) ** shard_levels(own_keys[12], (NJ,), ((0, 4),), -0.2, 0.2), -1.5, -0.3)
    return dict(amplitudes=amplitudes, integrals=integrals, row_intersection=row_intersection, column_intersection=column_intersection, row_tiles=row_tiles, row_coupling=row_coupling, row_counts=row_counts, column_tiles=column_tiles, column_coupling=column_coupling, column_counts=column_counts, virtual_energy=virtual_energy, first_energy=first_energy, second_energy=second_energy)


def sandwich(intersection, block):
    left = jnp.matmul(intersection, block, precision=lax.Precision.HIGHEST)
    return jnp.matmul(left, jnp.swapaxes(intersection, -1, -2), precision=lax.Precision.HIGHEST)


def reference(amplitudes, integrals, row_intersection, column_intersection, row_tiles, row_coupling, row_counts, column_tiles, column_coupling, column_counts, virtual_energy, first_energy, second_energy):
    denom = virtual_energy[:, :, :, None] + virtual_energy[:, :, None, :] - first_energy[:, None, None, None] - second_energy[None, :, None, None]
    slot_index = jnp.arange(row_tiles.shape[1], dtype=jnp.int32)
    row_weight = row_coupling * (slot_index[None, :] < row_counts[:, None]).astype(row_coupling.dtype)
    column_weight = column_coupling * (slot_index[None, :] < column_counts[:, None]).astype(column_coupling.dtype)
    current = amplitudes
    residual = jnp.zeros_like(amplitudes)
    for iteration in range(ITERS):
        def row_part(packed):
            tiles, weight, intersection = packed
            chosen = jnp.swapaxes(current[tiles], 0, 1)
            product = sandwich(intersection, chosen)
            return jnp.einsum('l,jlab->jab', weight, product, precision=lax.Precision.HIGHEST)

        def column_part(packed):
            own_row, intersection = packed
            chosen = own_row[column_tiles]
            product = sandwich(intersection, chosen)
            return jnp.einsum('jl,jlab->jab', column_weight, product, precision=lax.Precision.HIGHEST)

        row_term = lax.map(row_part, (row_tiles, row_weight, row_intersection))
        column_term = lax.map(column_part, (current, column_intersection))
        residual = integrals + denom * current - row_term - column_term
        current = current - residual / denom
    return current, residual
```

```python
import functools

import jax
import jax.numpy as jnp
from jax import lax
from jax.experimental import pallas as pl
from jax.experimental.pallas import tpu as pltpu
from jax.sharding import PartitionSpec as P

ITERS = 2
LANES = 128
F32, BF16 = jnp.float32, jnp.bfloat16
ANY = pl.BlockSpec(memory_space=pl.ANY)
SMEM = pl.BlockSpec(memory_space=pltpu.SMEM)
VMEM = pl.BlockSpec(memory_space=pltpu.VMEM)


class Packing:
    def __init__(self, tiles, side):
        self.tiles, self.side = tiles, side
        self.main = side // LANES * LANES
        self.tail = side - self.main
        self.across = LANES // self.tail if self.tail else 1
        while self.tail and (tiles * side % (self.across * 8) or side % (tiles * side // self.across)):
            self.across -= 1
        self.depth = tiles * side // self.across if self.tail else 0
        self.rows = tiles * side * (self.main // LANES) + self.depth
        self.fill = -3 * self.tail % LANES
        self.k = 3 * side + self.fill

    def write(self, ref, tile, block):
        for c in range(self.main // LANES):
            at = (tile * (self.main // LANES) + c) * self.side
            ref[at : at + self.side, :] = block[:, c * LANES : (c + 1) * LANES]
        if self.tail:
            top = self.tiles * self.side * (self.main // LANES)
            per = self.side // self.depth
            for r in range(per):
                a = tile * per + r
                ref[top : top + self.depth, a * self.tail : (a + 1) * self.tail] = block[
                    r * self.depth : (r + 1) * self.depth, self.main :
                ]

    def read(self, ref, lead, tile):
        groups = []
        for c in range(self.main // LANES):
            at = (tile * (self.main // LANES) + c) * self.side
            groups.append((c * LANES, ref[(*lead, slice(at, at + self.side), slice(None))]))
        if self.tail:
            top = self.tiles * self.side * (self.main // LANES)
            per = self.side // self.depth
            parts = []
            for r in range(per):
                a = tile * per + r
                parts.append(ref[(*lead, slice(top, top + self.depth), slice(a * self.tail, (a + 1) * self.tail))])
            groups.append((self.main, jnp.concatenate(parts, axis=0)))
        return groups


def halves(x):
    high = x.astype(BF16)
    return high, (x - high.astype(F32)).astype(BF16)


def spread(x, pack, order):
    main = halves(x[:, : pack.main]) if pack.main else None
    parts = [main[o] for o in order] if pack.main else []
    if pack.tail:
        tail = halves(x[:, pack.main :])
        wide = [tail[o].astype(F32) for o in order]
        if pack.fill:
            wide.append(jnp.zeros((x.shape[0], pack.fill), F32))
        parts.append(jnp.concatenate(wide, axis=1).astype(BF16))
    return jnp.concatenate(parts, axis=1)


def store_right(ref, at, groups, pack):
    main, tail = pack.main, pack.tail
    for first, x in groups:
        columns = slice(first, first + x.shape[1])
        high, low = halves(x)
        for p, half in enumerate((high, high, low)):
            if main:
                ref[at, p * main : (p + 1) * main, columns] = half[:main]
            if tail:
                ref[at, 3 * main + p * tail : 3 * main + (p + 1) * tail, columns] = half[main:]
        if pack.fill:
            ref[at, pack.k - pack.fill :, columns] = jnp.zeros((pack.fill, x.shape[1]), BF16)


def add_slots(total, at, count, slots, wait, source, weight, pack, right):
    def one(l, w):
        left = spread(slots(l), pack, (0, 1, 0))
        product = jnp.dot(left, right[source(l)], preferred_element_type=F32)
        return left, spread(w * product, pack, (0, 0, 1))

    def two(step, carry):
        l0 = 2 * step
        l1 = jnp.minimum(l0 + 1, count - 1)
        wait(l0)

        @pl.when(l0 + 1 < count)
        def _():
            wait(l1)

        s0, x0 = one(l0, weight(l0))
        s1, x1 = one(l1, jnp.where(l0 + 1 < count, weight(l1), 0.0))
        total[at] += lax.dot_general(
            jnp.concatenate([x0, x1], axis=1),
            jnp.concatenate([s0, s1], axis=1),
            (((1,), (1,)), ((), ())),
            preferred_element_type=F32,
        )
        return carry

    lax.fori_loop(0, (count + 1) // 2, two, 0)


def pack_kernel(pack, t_ref, *out_refs):
    joint, chunks = out_refs[0], out_refs[1:]
    for i, chunk in enumerate(chunks):
        for j in range(pack.tiles):
            pack.write(chunk, j, t_ref[i, j])
            pack.write(joint.at[i], j, t_ref[i, j])


def row_kernel(pack, n, tiles_ref, coupling_ref, counts_ref, s_ref, *refs):
    shards, (out, held, right, slots, sems, slot_sems) = refs[:n], refs[n:]
    rows, columns = s_ref.shape[0], s_ref.shape[1]
    me = lax.axis_index("ia")
    for r in range(n):
        pltpu.make_async_copy(shards[r], held.at[r], sems.at[r]).start()

    def slot_copy(i, j, l):
        return pltpu.make_async_copy(s_ref.at[i, j, l], slots.at[i, j, l], slot_sems.at[i, j, l])

    for i in range(rows):
        for j in range(columns):

            def begin(l, carry, i=i, j=j):
                slot_copy(i, j, l).start()
                return carry

            lax.fori_loop(0, counts_ref[i], begin, 0)
    out[...] = jnp.zeros(out.shape, F32)
    for r in range(n):
        pltpu.make_async_copy(shards[r], held.at[r], sems.at[r]).wait()

    def unpack(at, carry):
        r, i = at // rows, lax.rem(at, rows)
        for j in range(columns):
            store_right(right, at * columns + j, pack.read(held, (r, i), j), pack)
        return carry

    lax.fori_loop(0, n * rows, unpack, 0)
    for i in range(rows):
        for j in range(columns):

            def source(l, i=i, j=j):
                k = tiles_ref[i, l]
                return (((k // rows) ^ me) * rows + lax.rem(k, rows)) * columns + j

            add_slots(
                out.at[i],
                j,
                counts_ref[i],
                lambda l, i=i, j=j: slots[i, j, l],
                lambda l, i=i, j=j: slot_copy(i, j, l).wait(),
                source,
                lambda l, i=i: coupling_ref[i, l],
                pack,
                right,
            )


def column_kernel(pack, n, i, last, *refs):
    tiles_ref, coupling_ref, counts_ref, first_ref, second_ref, energy_ref, s_ref = refs[:7]
    row_ref, t_ref, integral_ref = refs[7:10]
    shards = refs[10 : 10 + n]
    rest = refs[10 + n :]
    if last and i > 0:
        rest = rest[2:]
    outs = 2
    out_refs, (held, right, slots, total, row, t, integral, sems, slot_sems) = rest[:outs], rest[outs:]
    columns = s_ref.shape[1]
    side = pack.side
    me = lax.axis_index("ja")
    for r in range(n):
        pltpu.make_async_copy(shards[r], held.at[r], sems.at[r]).start()

    def slot_copy(j, l):
        return pltpu.make_async_copy(s_ref.at[i, j, l], slots.at[j, l], slot_sems.at[j, l])

    for j in range(columns):

        def begin(l, carry, j=j):
            slot_copy(j, l).start()
            return carry

        lax.fori_loop(0, counts_ref[j], begin, 0)
    others = [
        pltpu.make_async_copy(row_ref.at[i], row, sems.at[n]),
        pltpu.make_async_copy(t_ref.at[i] if len(t_ref.shape) == 4 else t_ref, t, sems.at[n + 1]),
        pltpu.make_async_copy(integral_ref.at[i], integral, sems.at[n + 2]),
    ]
    for copy in others:
        copy.start()
    total[...] = jnp.zeros(total.shape, F32)
    for r in range(n):
        pltpu.make_async_copy(shards[r], held.at[r], sems.at[r]).wait()

    def unpack(r, carry):
        for j in range(columns):
            store_right(right, r * columns + j, pack.read(held, (r,), j), pack)
        return carry

    lax.fori_loop(0, n, unpack, 0)
    for j in range(columns):

        def source(l, j=j):
            k = tiles_ref[j, l]
            return ((k // columns) ^ me) * columns + lax.rem(k, columns)

        add_slots(
            total,
            j,
            counts_ref[j],
            lambda l, j=j: slots[j, l],
            lambda l, j=j: slot_copy(j, l).wait(),
            source,
            lambda l, j=j: coupling_ref[j, l],
            pack,
            right,
        )
    for copy in others:
        copy.wait()
    on_diagonal = lax.broadcasted_iota(jnp.int32, (side, side), 0) == lax.broadcasted_iota(
        jnp.int32, (side, side), 1
    )
    for j in range(columns):
        energy = jnp.broadcast_to(energy_ref[i, j : j + 1, :], (side, side))
        turned = jnp.sum(jnp.where(on_diagonal, energy, 0.0), axis=1, keepdims=True)
        denom = turned + energy - first_ref[i] - second_ref[j]
        residual = integral[j] + denom * t[j] - row[j] - total[j]
        new = t[j] - residual / denom
        if last:
            t[j] = new
            row[j] = residual
        else:
            out_refs[0][j] = new
            pack.write(out_refs[1], j, new)
    if last:
        copies = [
            pltpu.make_async_copy(t, out_refs[0].at[i], sems.at[n]),
            pltpu.make_async_copy(row, out_refs[1].at[i], sems.at[n + 1]),
        ]
        for copy in copies:
            copy.start()
        for copy in copies:
            copy.wait()
    return


def gather(x, axis, n, after=None):
    found = {0: x}
    bit = n // 2
    while bit:
        swap = [(d, d ^ bit) for d in range(n)]
        for r in list(found):
            found[r ^ bit] = lax.ppermute(found[r], axis, swap)
        bit //= 2
    return [found[r] for r in range(n)]


def local(
    n_row,
    n_column,
    amplitudes,
    integrals,
    row_intersection,
    column_intersection,
    row_tiles,
    row_coupling,
    row_counts,
    column_tiles,
    column_coupling,
    column_counts,
    virtual_energy,
    first_energy,
    second_energy,
):
    rows, columns, length, side = row_intersection.shape[:4]
    pack = Packing(columns, side)
    chunk_shape = jax.ShapeDtypeStruct((pack.rows, LANES), F32)
    pair_shape = jax.ShapeDtypeStruct((columns, side, side), F32)
    full_shape = jax.ShapeDtypeStruct((rows, columns, side, side), F32)
    params = pltpu.CompilerParams()

    def cost(slots):
        return pl.CostEstimate(
            flops=slots * 12 * side**3, bytes_accessed=slots * side * side * 4, transcendentals=0
        )

    packed = pl.pallas_call(
        functools.partial(pack_kernel, pack),
        out_shape=(jax.ShapeDtypeStruct((rows, pack.rows, LANES), F32),) + (chunk_shape,) * rows,
        in_specs=[VMEM],
        out_specs=(VMEM,) * (rows + 1),
        compiler_params=params,
        name="pack",
    )(amplitudes)
    joint, chunks = packed[0], list(packed[1:])

    def row_terms(shards):
        return pl.pallas_call(
            functools.partial(row_kernel, pack, n_row),
            out_shape=full_shape,
            in_specs=[SMEM] * 3 + [ANY] * (1 + n_row),
            out_specs=VMEM,
            scratch_shapes=[
                pltpu.VMEM((n_row, rows, pack.rows, LANES), F32),
                pltpu.VMEM((n_row * rows * columns, pack.k, side), BF16),
                pltpu.VMEM((rows, columns, length, side, side), F32),
                pltpu.SemaphoreType.DMA((n_row,)),
                pltpu.SemaphoreType.DMA((rows, columns, length)),
            ],
            compiler_params=params,
            cost_estimate=cost(rows * columns * length),
            name="row_terms",
        )(row_tiles, row_coupling, row_counts, row_intersection, *shards)

    def column_step(i, last, row_term, current, shards, outputs):
        c_length = column_intersection.shape[2]
        if last:
            out_shape, out_specs = (full_shape, full_shape), (ANY, ANY)
        else:
            out_shape, out_specs = (pair_shape, chunk_shape), (VMEM, VMEM)
        extra = list(outputs) if last and i > 0 else []
        return pl.pallas_call(
            functools.partial(column_kernel, pack, n_column, i, last),
            out_shape=out_shape,
            in_specs=[SMEM] * 5 + [VMEM] + [ANY] * (4 + n_column + len(extra)),
            out_specs=out_specs,
            scratch_shapes=[
                pltpu.VMEM((n_column, pack.rows, LANES), F32),
                pltpu.VMEM((n_column * columns, pack.k, side), BF16),
                pltpu.VMEM((columns, c_length, side, side), F32),
                pltpu.VMEM((columns, side, side), F32),
                pltpu.VMEM((columns, side, side), F32),
                pltpu.VMEM((columns, side, side), F32),
                pltpu.VMEM((columns, side, side), F32),
                pltpu.SemaphoreType.DMA((n_column + 3,)),
                pltpu.SemaphoreType.DMA((columns, c_length)),
            ],
            input_output_aliases={10 + n_column + e: e for e in range(len(extra))},
            compiler_params=params,
            cost_estimate=cost(columns * c_length),
            name=f"column_step_{i}",
        )(
            column_tiles,
            column_coupling,
            column_counts,
            first_energy,
            second_energy,
            virtual_energy,
            column_intersection,
            row_term,
            current,
            integrals,
            *shards,
            *extra,
        )

    currents = [amplitudes] * rows
    outputs = ()
    for iteration in range(ITERS):
        last = iteration == ITERS - 1
        across = [gather(chunk, "ja", n_column) for chunk in chunks]
        if iteration == 0:
            row_shards = gather(joint, "ia", n_row)
        else:
            row_shards = gather(jnp.stack(chunks), "ia", n_row)
        row_term = row_terms(row_shards)
        results = []
        for i in range(rows):
            outputs = column_step(i, last, row_term, currents[i], across[i], outputs)
            results.append(outputs)
        if not last:
            currents = [r[0] for r in results]
            chunks = [r[1] for r in results]
    return outputs


def solution(mesh):
    placed = (
        P(("grp", "ia"), "ja", None, None),
        P(("grp", "ia"), "ja", None, None),
        P(("grp", "ia"), "ja", None, None, None),
        P(("grp", "ia"), "ja", None, None, None),
        P(("grp", "ia"), None),
        P(("grp", "ia"), None),
        P(("grp", "ia")),
        P(("grp", "ja"), None),
        P(("grp", "ja"), None),
        P(("grp", "ja")),
        P(("grp", "ia"), "ja", None),
        P(("grp", "ia")),
        P(("grp", "ja")),
    )
    return jax.shard_map(
        functools.partial(local, mesh.shape["ia"], mesh.shape["ja"]),
        mesh=mesh,
        in_specs=placed,
        out_specs=(P(("grp", "ia"), "ja", None, None), P(("grp", "ia"), "ja", None, None)),
        check_vma=False,
    )
```
